32 devices in a mesh: row: 4 (over x, core), col: 8 (over z, y).
Axes of the slice: x: 2, y: 2, z: 4, core: 2. Of those that a mesh axis runs over, the one named last changes fastest.
Arguments:
- adjacency_tiles: bfloat16 [4, 8, 80, 128, 128], P('row', 'col'), may hold values from -0.09375 to 0.09375
- tile_rows: int32 [4, 8, 80], P('row', 'col'), may hold values from 0 to 15, as said below
- tile_cols: int32 [4, 8, 80], P('row', 'col'), may hold values from 0 to 7, as said below
- tile_counts: int32 [4, 8], P('row', 'col'), may hold values from 40 to 80, as said below
- features: bfloat16 [8192, 1024], P('col', 'row'), may hold values from -6 to 6
- weight: bfloat16 [1024, 1024], P('col'), may hold values from -0.1875 to 0.1875
Outputs:
- activated: bfloat16 [8192, 1024], P(('row', 'col'))
The draws below stay inside these ranges and needn't reach their ends.
Inputs may be any that keep to these rules, and one draw needn't show every extreme that they name: `tile_counts`: some grid cell holds exactly 80 live tiles in every draw. In each grid cell the first tile_counts entries of tile_rows and tile_cols name distinct (row, column) tile pairs; later entries are valid indices but unused. `tile_cols`: see tile_rows.
All inputs are finite; a program needn't handle non-finite values.
Results may differ from the reference program's by a relative error of at most 0.014.
Values may be sent and summed in bfloat16 or wider, within the bound.
A program may use at most 64 MiB of HBM per device.

```python
import jax
import jax.numpy as jnp
from jax import lax

F = 1024
TB = 128
CB_DEV = 8
CAP = 80
RB_DEV = 16
NODES = 8192
N_ROW = 4
N_COL = 8


def layout_draw(key):
    base = jax.random.fold_in(key, 7)
    key_first, key_busy, key_slots = jax.random.split(base, 3)
    cells = N_ROW * N_COL
    lowest = CAP // 2
    counts = jax.random.randint(key_first, (N_ROW, N_COL), lowest, CAP + 1)
    busiest = jax.random.randint(key_busy, (), 0, cells)
    flat_index = jnp.arange(cells).reshape(N_ROW, N_COL)
    counts = jnp.where(flat_index == busiest, CAP, counts)
    slot_keys = jax.random.split(key_slots, cells)
    orders = jax.vmap(lambda single: jax.random.permutation(single, RB_DEV * CB_DEV)[:CAP])(slot_keys)
    orders = orders.reshape(N_ROW, N_COL, CAP)
    return (counts.astype(jnp.int32), (orders // CB_DEV).astype(jnp.int32), (orders % CB_DEV).astype(jnp.int32))


def draw_tile_rows(key, part):
    return layout_draw(key)[1]


def draw_tile_cols(key, part):
    return layout_draw(key)[2]


def draw_tile_counts(key, part):
    return layout_draw(key)[0]


def level_of(key, shape, cuts, smallest, high):
    def one(position, shards_of):
        draws = jax.random.uniform(jax.random.fold_in(jax.random.fold_in(key, 6), position), (shards_of,), jnp.float32, smallest / len(cuts), high / len(cuts))
        return jnp.repeat(jnp.exp(draws), shape[position] // shards_of).reshape((-1,) + (1,) * (len(shape) - position - 1))

    gain = one(*cuts[0])
    for cut in cuts[1:]:
        gain = gain * one(*cut)
    return gain


def scatter_about(key, dims, scale, limit, shards=(), kind=jnp.bfloat16):
    array = scale * jax.random.normal(key, dims, jnp.float32)
    if shards:
        array = array * level_of(key, dims, shards, -0.22, 0.18)
    return jnp.clip(array, -limit, limit).astype(kind)


def setup_inputs(seed: int = 0) -> dict:
    streams_of = jax.random.split(jax.random.key(seed), 7)
    adjacency_tiles = scatter_about(streams_of[0], (N_ROW, N_COL, CAP, TB, TB), (TB * CAP * N_COL * 3 // (4 * RB_DEV)) ** -0.5, 0.09375, ((0, 4), (1, 8)))
    tile_rows = draw_tile_rows(jax.random.fold_in(streams_of[6], 71), 0)
    tile_cols = draw_tile_cols(jax.random.fold_in(streams_of[6], 71), 0)
    tile_counts = draw_tile_counts(jax.random.fold_in(streams_of[6], 71), 0)
    features = scatter_about(streams_of[4], (NODES, F), 1.0, 6.0, ((0, 8), (1, 4)))
    weight = scatter_about(streams_of[5], (F, F), F ** -0.5, 0.1875, ((0, 8),))
    return dict(adjacency_tiles=adjacency_tiles, tile_rows=tile_rows, tile_cols=tile_cols, tile_counts=tile_counts, features=features, weight=weight)


def accumulate(adjacency_tiles, tile_rows, tile_cols, tile_count, feature_blocks, row_blocks):
    tile_edge = adjacency_tiles.shape[1]
    panel_width = feature_blocks.shape[2]
    group_count = (tile_count + 7) // 8

    def add_group(group_index, totals):
        for member in range(8):
            slot_index = group_index * 8 + member
            one_tile = lax.dynamic_index_in_dim(adjacency_tiles, slot_index, 0, keepdims=False)
            row_block = tile_rows[slot_index]
            col_block = tile_cols[slot_index]
            source = lax.dynamic_index_in_dim(feature_blocks, col_block, 0, keepdims=False)
            product = jnp.dot(one_tile, source, preferred_element_type=jnp.float32)
            is_live = (slot_index < tile_count).astype(jnp.float32)
            current = lax.dynamic_index_in_dim(totals, row_block, 0, keepdims=True)
            totals = lax.dynamic_update_index_in_dim(totals, current + is_live * product[None], row_block, 0)
        return totals

    start_totals = jnp.zeros((row_blocks, tile_edge, panel_width), jnp.float32)
    return lax.fori_loop(jnp.int32(0), group_count.astype(jnp.int32), add_group, start_totals)


def reference(adjacency_tiles, tile_rows, tile_cols, tile_counts, features, weight):
    feature_all = features.reshape(N_COL, CB_DEV, TB, F)

    def row_stripe(row_index):
        def add_column(running, col_index):
            partial_value = accumulate(adjacency_tiles[row_index, col_index], tile_rows[row_index, col_index],
                                 tile_cols[row_index, col_index], tile_counts[row_index, col_index],
                                 feature_all[col_index], RB_DEV)
            rounded = lax.optimization_barrier(partial_value.astype(jnp.bfloat16))
            return running + rounded.astype(jnp.float32), None

        running, unused = lax.scan(add_column, jnp.zeros((RB_DEV, TB, F), jnp.float32),
                                   jnp.arange(N_COL, dtype=jnp.int32))
        return running.reshape(RB_DEV * TB, F)

    aggregated = lax.map(row_stripe, jnp.arange(N_ROW, dtype=jnp.int32)).reshape(NODES, F).astype(jnp.bfloat16)
    hidden = jnp.dot(aggregated, weight, preferred_element_type=jnp.float32)
    return jnp.maximum(hidden, 0.0).astype(jnp.bfloat16)
```

```python
import functools

import jax
import jax.numpy as jnp
from jax import lax
from jax.experimental import pallas as pl
from jax.experimental.pallas import tpu as pltpu
from jax.sharding import PartitionSpec as P

MESH = pl.DeviceIdType.MESH


def densify(adjacency_tiles, tile_rows, tile_cols, tile_count, row_blocks, column_blocks):
    slots = adjacency_tiles.shape[0]
    tile_edge = adjacency_tiles.shape[1]
    live_mask = (jnp.arange(slots, dtype=jnp.int32) < tile_count).astype(jnp.bfloat16)
    masked = adjacency_tiles * live_mask[:, None, None]
    grid = jnp.zeros((row_blocks, column_blocks, tile_edge, tile_edge), jnp.bfloat16)
    grid = grid.at[tile_rows, tile_cols].add(masked)
    return grid.transpose(0, 2, 1, 3).reshape(row_blocks * tile_edge, column_blocks * tile_edge)


def reduce_whole(partial_rows):
    return lax.psum_scatter(
        partial_rows.astype(jnp.bfloat16), "col", scatter_dimension=0, tiled=True
    ).astype(jnp.float32)


def shards(adjacency_tiles, tile_rows, tile_cols, tile_counts, features, weight):
    local_tiles = adjacency_tiles[0, 0]
    local_rows = tile_rows[0, 0]
    local_cols = tile_cols[0, 0]
    local_count = tile_counts[0, 0]
    tile_edge = local_tiles.shape[1]
    column_blocks = features.shape[0] // tile_edge
    row_blocks = column_blocks * lax.axis_size("col") // lax.axis_size("row")
    dense_block = densify(
        local_tiles, local_rows, local_cols, local_count, row_blocks, column_blocks
    )
    whole = lax.all_gather(features, "row", axis=1, tiled=True)
    partial_value = jnp.dot(dense_block, whole, preferred_element_type=jnp.float32)
    summed = reduce_whole(partial_value.astype(jnp.bfloat16).astype(jnp.float32))
    aggregated = summed.astype(jnp.bfloat16)
    full_weight = lax.all_gather(weight, "col", axis=0, tiled=True)
    hidden = jnp.dot(aggregated, full_weight, preferred_element_type=jnp.float32)
    return jnp.maximum(hidden, 0.0).astype(jnp.bfloat16)


def layer_kernel(
    inv, adj_hbm, feat_hbm, w_hbm, out_ref,
    adj, dense, feat, wfull, psend, own, yr, zr, acc, hidden,
    lsem, fsend, frecv, wsend, wrecv, vsend, vrecv, ysend, yrecv, zsend, zrecv,
):
    p, q = lax.axis_index("row"), lax.axis_index("col")
    y, z = q % 2, q // 2
    mate = p + 1 - 2 * (p % 2)
    across = (p + 2) % 4
    slots = adj_hbm.shape[0]
    tb = adj_hbm.shape[1]
    quarter = wfull.shape[2]

    cp_adj = pltpu.make_async_copy(adj_hbm, adj.at[pl.ds(0, slots)], lsem.at[0])
    cp_adj.start()
    cp_feat = pltpu.make_async_copy(feat_hbm, feat.at[0], lsem.at[1])
    cp_feat.start()
    w_mine = w_hbm.at[pl.ds(pl.multiple_of(p * quarter, quarter), quarter)]
    cp_w = pltpu.make_async_copy(w_mine, wfull.at[q, p], lsem.at[2])
    cp_w.start()

    barrier = pltpu.get_barrier_semaphore()
    for step in range(1, 8):
        pl.semaphore_signal(barrier, inc=1, device_id={"col": (q + step) % 8}, device_id_type=MESH)
    pl.semaphore_signal(barrier, inc=1, device_id={"row": mate}, device_id_type=MESH)
    pl.semaphore_signal(barrier, inc=1, device_id={"row": across}, device_id_type=MESH)
    pl.semaphore_wait(barrier, 9)

    def row_copy(src, dst, ssem, rsem, to):
        return pltpu.make_async_remote_copy(
            src_ref=src, dst_ref=dst, send_sem=ssem, recv_sem=rsem,
            device_id={"row": to}, device_id_type=MESH)

    def col_copy(src, dst, ssem, rsem, to):
        return pltpu.make_async_remote_copy(
            src_ref=src, dst_ref=dst, send_sem=ssem, recv_sem=rsem,
            device_id={"col": to}, device_id_type=MESH)

    f_mate = row_copy(feat_hbm, feat.at[1], fsend.at[0], frecv.at[0], mate)
    f_across = row_copy(feat_hbm, feat.at[2], fsend.at[1], frecv.at[1], across)
    f_fwd = row_copy(feat.at[2], feat.at[3], fsend.at[2], frecv.at[2], mate)
    f_mate.start()
    f_across.start()
    w_out = [
        col_copy(w_mine, wfull.at[q, p], wsend.at[step - 1], wrecv.at[step - 1], (q + step) % 8)
        for step in range(1, 8)
    ]
    for copy in w_out:
        copy.start()
    v_mate = row_copy(wfull.at[:, p], wfull.at[:, p], vsend.at[0], vrecv.at[0], mate)
    v_across = row_copy(wfull.at[:, p], wfull.at[:, p], vsend.at[1], vrecv.at[1], across)
    v_fwd = row_copy(wfull.at[:, across], wfull.at[:, across], vsend.at[2], vrecv.at[2], mate)

    adj[slots] = jnp.zeros((tb, tb), jnp.bfloat16)
    cp_adj.wait()

    @pl.loop(0, 8)
    def _(chunk):
        for half in range(2):
            for cb in range(8):
                dense[chunk, half * tb:(half + 1) * tb, cb * tb:(cb + 1) * tb] = adj[
                    inv[chunk * 16 + half * 8 + cb]]

    power = (1 + 3 * (z % 2)) * (1 + 15 * (z // 2))

    def dest(step):
        code = 15 * ((3 - step) // 3) + 114 * ((step % 3) % 2) + 153 * ((step % 3) // 2)
        code = code + 228 * (step // 3)
        return (code // power) % 4

    def y_copy(k, d):
        return col_copy(psend.at[k, d], yr.at[k, d], ysend.at[k, d], yrecv.at[k, d], 2 * z + 1 - y)

    def z_copy(k, d):
        side = (d - z + 4) // 4
        return col_copy(own.at[k, d], zr.at[side, k, d], zsend.at[k, d], zrecv.at[side, k, d],
                        q + 4 * side - 2)

    def product(k, chunk):
        return jnp.dot(dense[chunk], feat[k], preferred_element_type=jnp.float32)

    def compute(k):
        @pl.loop(0, 4)
        def _(step):
            d = dest(step)
            psend[k, d] = product(k, 2 * d + 1 - y).astype(jnp.bfloat16)
            y_copy(k, d).start()

        @pl.loop(0, 4)
        def _(step):
            d = dest(step)
            own[k, d] = product(k, 2 * d + y).astype(jnp.bfloat16)

    def reduce(k):
        @pl.loop(0, 3)
        def _(step):
            d = dest(step)
            side = (d - z + 4) // 4
            up = z + 1 - 2 * side
            y_copy(k, d).wait_recv()
            has_up = (up + 1) % 5 > 0

            @pl.when(has_up)
            def _():
                z_copy(k, d).wait_recv()
                own[k, d] = (own[k, d].astype(jnp.float32) + yr[k, d].astype(jnp.float32)
                             + zr[side, k, d].astype(jnp.float32)).astype(jnp.bfloat16)

            @pl.when(jnp.logical_not(has_up))
            def _():
                own[k, d] = (own[k, d].astype(jnp.float32)
                             + yr[k, d].astype(jnp.float32)).astype(jnp.bfloat16)

            z_copy(k, d).start()

        y_copy(k, z).wait_recv()
        acc[...] = own[k, z].astype(jnp.float32) + yr[k, z].astype(jnp.float32)

        for side in (0, 1):
            @pl.when(z < 3 if side == 0 else z > 0)
            def _():
                col_copy(own.at[k, z], zr.at[side, k, z], zsend.at[k, z], zrecv.at[side, k, z],
                         2 * z + 1 - y).wait_recv()
                acc[...] += zr[side, k, z].astype(jnp.float32)

    panels = (p, mate, across, (mate + 2) % 4)

    def finish(k):
        rows = wfull[pl.ds(2 * panels[k], 2)].reshape(8 * quarter, wfull.shape[3])
        term = jnp.dot(acc[...].astype(jnp.bfloat16), rows, preferred_element_type=jnp.float32)
        if k == 0:
            hidden[...] = term
        elif k < 3:
            hidden[...] += term
        else:
            out_ref[...] = jnp.maximum(hidden[...] + term, 0.0).astype(jnp.bfloat16)

    cp_feat.wait()
    compute(0)
    f_mate.wait_recv()
    compute(1)
    cp_w.wait()
    for copy in w_out:
        copy.wait_recv()
    f_across.wait_recv()
    f_fwd.start()
    v_mate.start()
    v_across.start()
    reduce(0)
    compute(2)
    v_across.wait_recv()
    v_fwd.start()
    v_mate.wait_recv()
    v_fwd.wait_recv()
    finish(0)
    reduce(1)
    finish(1)
    f_fwd.wait_recv()
    compute(3)
    reduce(2)
    finish(2)
    reduce(3)
    finish(3)

    for copy in [f_mate, f_across, f_fwd, v_mate, v_across, v_fwd] + w_out:
        copy.wait_send()
    for k in range(4):
        @pl.loop(0, 4)
        def _(step):
            y_copy(k, dest(step)).wait_send()

        @pl.loop(0, 3)
        def _(step):
            z_copy(k, dest(step)).wait_send()


def fused_shards(adjacency_tiles, tile_rows, tile_cols, tile_counts, features, weight):
    tiles = adjacency_tiles[0, 0]
    slots, tb = tiles.shape[:2]
    live = jnp.arange(slots, dtype=jnp.int32)
    key = tile_rows[0, 0] * 8 + tile_cols[0, 0]
    place = jnp.arange(128, dtype=jnp.int32)
    hit = (place[:, None] == key[None, :]) & (live[None, :] < tile_counts[0, 0])
    inv = jnp.min(jnp.where(hit, live[None, :], slots), axis=1)
    width = features.shape[1]
    wide = weight.shape[1]
    bf = jnp.bfloat16
    dma = pltpu.SemaphoreType.DMA
    blocks = (4, 4, 256, width)
    return pl.pallas_call(
        layer_kernel,
        out_shape=jax.ShapeDtypeStruct((256, wide), bf),
        in_specs=[pl.BlockSpec(memory_space=pltpu.SMEM)]
        + [pl.BlockSpec(memory_space=pl.ANY)] * 3,
        out_specs=pl.BlockSpec(memory_space=pltpu.VMEM),
        scratch_shapes=[
            pltpu.VMEM((slots + 1, tb, tb), bf),
            pltpu.VMEM((8, 256, 1024), bf),
            pltpu.VMEM((4, 1024, width), bf),
            pltpu.VMEM((8, 4, weight.shape[0] // 4, wide), bf),
            pltpu.VMEM(blocks, bf),
            pltpu.VMEM(blocks, bf),
            pltpu.VMEM(blocks, bf),
            pltpu.VMEM((2,) + blocks, bf),
            pltpu.VMEM((256, width), jnp.float32),
            pltpu.VMEM((256, wide), jnp.float32),
            dma((3,)),
            dma((3,)), dma((3,)),
            dma((7,)), dma((7,)),
            dma((3,)), dma((3,)),
            dma((4, 4)), dma((4, 4)),
            dma((4, 4)), dma((2, 4, 4)),
        ],
        compiler_params=pltpu.CompilerParams(
            collective_id=0, has_side_effects=True, vmem_limit_bytes=48 * 2**20),
    )(inv, tiles, features, weight)


def solution(mesh):
    fits = mesh.shape["row"] == 4 and mesh.shape["col"] == 8
    return jax.shard_map(
        fused_shards if fits else shards,
        mesh=mesh,
        in_specs=(
            P("row", "col", None, None, None),
            P("row", "col", None),
            P("row", "col", None),
            P("row", "col"),
            P("col", "row"),
            P("col", None),
        ),
        out_specs=P(("row", "col"), None),
        check_vma=False,
    )
```

```python
import functools

import jax
import jax.numpy as jnp
from jax import lax
from jax.experimental import pallas as pl
from jax.experimental.pallas import tpu as pltpu
from jax.sharding import PartitionSpec as P

MESH = pl.DeviceIdType.MESH


def densify(adjacency_tiles, tile_rows, tile_cols, tile_count, row_blocks, column_blocks):
    slots = adjacency_tiles.shape[0]
    tile_edge = adjacency_tiles.shape[1]
    live_mask = (jnp.arange(slots, dtype=jnp.int32) < tile_count).astype(jnp.bfloat16)
    masked = adjacency_tiles * live_mask[:, None, None]
    grid = jnp.zeros((row_blocks, column_blocks, tile_edge, tile_edge), jnp.bfloat16)
    grid = grid.at[tile_rows, tile_cols].add(masked)
    return grid.transpose(0, 2, 1, 3).reshape(row_blocks * tile_edge, column_blocks * tile_edge)


def reduce_whole(partial_rows):
    return lax.psum_scatter(
        partial_rows.astype(jnp.bfloat16), "col", scatter_dimension=0, tiled=True
    ).astype(jnp.float32)


def shards(adjacency_tiles, tile_rows, tile_cols, tile_counts, features, weight):
    local_tiles = adjacency_tiles[0, 0]
    local_rows = tile_rows[0, 0]
    local_cols = tile_cols[0, 0]
    local_count = tile_counts[0, 0]
    tile_edge = local_tiles.shape[1]
    column_blocks = features.shape[0] // tile_edge
    row_blocks = column_blocks * lax.axis_size("col") // lax.axis_size("row")
    dense_block = densify(
        local_tiles, local_rows, local_cols, local_count, row_blocks, column_blocks
    )
    whole = lax.all_gather(features, "row", axis=1, tiled=True)
    partial_value = jnp.dot(dense_block, whole, preferred_element_type=jnp.float32)
    summed = reduce_whole(partial_value.astype(jnp.bfloat16).astype(jnp.float32))
    aggregated = summed.astype(jnp.bfloat16)
    full_weight = lax.all_gather(weight, "col", axis=0, tiled=True)
    hidden = jnp.dot(aggregated, full_weight, preferred_element_type=jnp.float32)
    return jnp.maximum(hidden, 0.0).astype(jnp.bfloat16)


def layer_kernel(
    inv, adj_hbm, feat_hbm, w_hbm, out_ref,
    adj, dense, feat, wfull, psend, own, yr, zr, acc, hidden,
    lsem, fsend, frecv, wsend, wrecv, vsend, vrecv, ysend, yrecv, zsend, zrecv,
):
    p, q = lax.axis_index("row"), lax.axis_index("col")
    y, z = q % 2, q // 2
    mate = p + 1 - 2 * (p % 2)
    across = (p + 2) % 4
    slots = adj_hbm.shape[0]
    tb = adj_hbm.shape[1]
    quarter = wfull.shape[2]

    cp_adj = pltpu.make_async_copy(adj_hbm, adj.at[pl.ds(0, slots)], lsem.at[0])
    cp_adj.start()
    cp_feat = pltpu.make_async_copy(feat_hbm, feat.at[0], lsem.at[1])
    cp_feat.start()
    w_mine = w_hbm.at[pl.ds(pl.multiple_of(p * quarter, quarter), quarter)]
    cp_w = pltpu.make_async_copy(w_mine, wfull.at[q, p], lsem.at[2])
    cp_w.start()

    barrier = pltpu.get_barrier_semaphore()
    for step in range(1, 8):
        pl.semaphore_signal(barrier, inc=1, device_id={"col": (q + step) % 8}, device_id_type=MESH)
    pl.semaphore_signal(barrier, inc=1, device_id={"row": mate}, device_id_type=MESH)
    pl.semaphore_signal(barrier, inc=1, device_id={"row": across}, device_id_type=MESH)
    pl.semaphore_wait(barrier, 9)

    def row_copy(src, dst, ssem, rsem, to):
        return pltpu.make_async_remote_copy(
            src_ref=src, dst_ref=dst, send_sem=ssem, recv_sem=rsem,
            device_id={"row": to}, device_id_type=MESH)

    def col_copy(src, dst, ssem, rsem, to):
        return pltpu.make_async_remote_copy(
            src_ref=src, dst_ref=dst, send_sem=ssem, recv_sem=rsem,
            device_id={"col": to}, device_id_type=MESH)

    f_mate = row_copy(feat_hbm, feat.at[1], fsend.at[0], frecv.at[0], mate)
    f_across = row_copy(feat_hbm, feat.at[2], fsend.at[1], frecv.at[1], across)
    f_fwd = row_copy(feat.at[2], feat.at[3], fsend.at[2], frecv.at[2], mate)
    f_mate.start()
    f_across.start()
    w_out = [
        col_copy(w_mine, wfull.at[q, p], wsend.at[step - 1], wrecv.at[step - 1], (q + step) % 8)
        for step in range(1, 8)
    ]
    for copy in w_out:
        copy.start()
    v_mate = row_copy(wfull.at[:, p], wfull.at[:, p], vsend.at[0], vrecv.at[0], mate)
    v_across = row_copy(wfull.at[:, p], wfull.at[:, p], vsend.at[1], vrecv.at[1], across)
    v_fwd = row_copy(wfull.at[:, across], wfull.at[:, across], vsend.at[2], vrecv.at[2], mate)

    adj[slots] = jnp.zeros((tb, tb), jnp.bfloat16)
    cp_adj.wait()

    @pl.loop(0, 8)
    def _(chunk):
        for half in range(2):
            for cb in range(8):
                dense[chunk, half * tb:(half + 1) * tb, cb * tb:(cb + 1) * tb] = adj[
                    inv[chunk * 16 + half * 8 + cb]]

    power = (1 + 3 * (z % 2)) * (1 + 15 * (z // 2))

    def dest(step):
        code = 15 * ((3 - step) // 3) + 90 * ((step % 3) % 2) + 177 * ((step % 3) // 2)
        code = code + 228 * (step // 3)
        return (code // power) % 4

    def y_copy(k, d):
        return col_copy(psend.at[k, d], yr.at[k, d], ysend.at[k, d], yrecv.at[k, d], 2 * z + 1 - y)

    def z_copy(k, d):
        side = (d - z + 4) // 4
        return col_copy(own.at[k, d], zr.at[side, k, d], zsend.at[k, d], zrecv.at[side, k, d],
                        q + 4 * side - 2)

    def product(k, chunk):
        return jnp.dot(dense[chunk], feat[k], preferred_element_type=jnp.float32)

    def compute(k):
        @pl.loop(0, 4)
        def _(step):
            d = dest(step)
            psend[k, d] = product(k, 2 * d + 1 - y).astype(jnp.bfloat16)
            y_copy(k, d).start()

        @pl.loop(0, 4)
        def _(step):
            d = dest(step)
            own[k, d] = product(k, 2 * d + y).astype(jnp.bfloat16)

    def reduce(k, step):
        d = dest(step)
        side = (d - z + 4) // 4
        up = z + 1 - 2 * side
        y_copy(k, d).wait_recv()
        has_up = (up + 1) % 5 > 0

        @pl.when(has_up)
        def _():
            z_copy(k, d).wait_recv()
            own[k, d] = (own[k, d].astype(jnp.float32) + yr[k, d].astype(jnp.float32)
                         + zr[side, k, d].astype(jnp.float32)).astype(jnp.bfloat16)

        @pl.when(jnp.logical_not(has_up))
        def _():
            own[k, d] = (own[k, d].astype(jnp.float32)
                         + yr[k, d].astype(jnp.float32)).astype(jnp.bfloat16)

        z_copy(k, d).start()

    def settle(k):
        y_copy(k, z).wait_recv()
        acc[...] = own[k, z].astype(jnp.float32) + yr[k, z].astype(jnp.float32)

        for side in (0, 1):
            @pl.when(z < 3 if side == 0 else z > 0)
            def _():
                col_copy(own.at[k, z], zr.at[side, k, z], zsend.at[k, z], zrecv.at[side, k, z],
                         2 * z + 1 - y).wait_recv()
                acc[...] += zr[side, k, z].astype(jnp.float32)

    panels = (p, mate, across, (mate + 2) % 4)

    def finish(k):
        rows = wfull[pl.ds(2 * panels[k], 2)].reshape(8 * quarter, wfull.shape[3])
        term = jnp.dot(acc[...].astype(jnp.bfloat16), rows, preferred_element_type=jnp.float32)
        if k == 0:
            hidden[...] = term
        elif k < 3:
            hidden[...] += term
        else:
            out_ref[...] = jnp.maximum(hidden[...] + term, 0.0).astype(jnp.bfloat16)

    cp_feat.wait()
    compute(0)
    f_mate.wait_recv()
    compute(1)
    cp_w.wait()
    for copy in w_out:
        copy.wait_recv()
    f_across.wait_recv()
    f_fwd.start()
    v_mate.start()
    v_across.start()
    for step in range(3):
        reduce(0, step)
    compute(2)
    v_across.wait_recv()
    v_fwd.start()
    reduce(1, 0)
    settle(0)
    v_mate.wait_recv()
    v_fwd.wait_recv()
    finish(0)
    reduce(1, 1)
    reduce(1, 2)
    f_fwd.wait_recv()
    compute(3)
    reduce(2, 0)
    settle(1)
    finish(1)
    reduce(2, 1)
    reduce(2, 2)
    reduce(3, 0)
    settle(2)
    finish(2)
    reduce(3, 1)
    reduce(3, 2)
    settle(3)
    finish(3)

    for copy in [f_mate, f_across, f_fwd, v_mate, v_across, v_fwd] + w_out:
        copy.wait_send()
    for k in range(4):
        @pl.loop(0, 4)
        def _(step):
            y_copy(k, dest(step)).wait_send()

        @pl.loop(0, 3)
        def _(step):
            z_copy(k, dest(step)).wait_send()


def fused_shards(adjacency_tiles, tile_rows, tile_cols, tile_counts, features, weight):
    tiles = adjacency_tiles[0, 0]
    slots, tb = tiles.shape[:2]
    live = jnp.arange(slots, dtype=jnp.int32)
    key = tile_rows[0, 0] * 8 + tile_cols[0, 0]
    place = jnp.arange(128, dtype=jnp.int32)
    hit = (place[:, None] == key[None, :]) & (live[None, :] < tile_counts[0, 0])
    inv = jnp.min(jnp.where(hit, live[None, :], slots), axis=1)
    width = features.shape[1]
    wide = weight.shape[1]
    bf = jnp.bfloat16
    dma = pltpu.SemaphoreType.DMA
    blocks = (4, 4, 256, width)
    return pl.pallas_call(
        layer_kernel,
        out_shape=jax.ShapeDtypeStruct((256, wide), bf),
        in_specs=[pl.BlockSpec(memory_space=pltpu.SMEM)]
        + [pl.BlockSpec(memory_space=pl.ANY)] * 3,
        out_specs=pl.BlockSpec(memory_space=pltpu.VMEM),
        scratch_shapes=[
            pltpu.VMEM((slots + 1, tb, tb), bf),
            pltpu.VMEM((8, 256, 1024), bf),
            pltpu.VMEM((4, 1024, width), bf),
            pltpu.VMEM((8, 4, weight.shape[0] // 4, wide), bf),
            pltpu.VMEM(blocks, bf),
            pltpu.VMEM(blocks, bf),
            pltpu.VMEM(blocks, bf),
            pltpu.VMEM((2,) + blocks, bf),
            pltpu.VMEM((256, width), jnp.float32),
            pltpu.VMEM((256, wide), jnp.float32),
            dma((3,)),
            dma((3,)), dma((3,)),
            dma((7,)), dma((7,)),
            dma((3,)), dma((3,)),
            dma((4, 4)), dma((4, 4)),
            dma((4, 4)), dma((2, 4, 4)),
        ],
        compiler_params=pltpu.CompilerParams(
            collective_id=0, has_side_effects=True, vmem_limit_bytes=48 * 2**20),
    )(inv, tiles, features, weight)


def solution(mesh):
    fits = mesh.shape["row"] == 4 and mesh.shape["col"] == 8
    return jax.shard_map(
        fused_shards if fits else shards,
        mesh=mesh,
        in_specs=(
            P("row", "col", None, None, None),
            P("row", "col", None),
            P("row", "col", None),
            P("row", "col"),
            P("col", "row"),
            P("col", None),
        ),
        out_specs=P(("row", "col"), None),
        check_vma=False,
    )
```

```python
import functools

import jax
import jax.numpy as jnp
from jax import lax
from jax.experimental import pallas as pl
from jax.experimental.pallas import tpu as pltpu
from jax.sharding import PartitionSpec as P

MESH = pl.DeviceIdType.MESH


def densify(adjacency_tiles, tile_rows, tile_cols, tile_count, row_blocks, column_blocks):
    slots = adjacency_tiles.shape[0]
    tile_edge = adjacency_tiles.shape[1]
    live_mask = (jnp.arange(slots, dtype=jnp.int32) < tile_count).astype(jnp.bfloat16)
    masked = adjacency_tiles * live_mask[:, None, None]
    grid = jnp.zeros((row_blocks, column_blocks, tile_edge, tile_edge), jnp.bfloat16)
    grid = grid.at[tile_rows, tile_cols].add(masked)
    return grid.transpose(0, 2, 1, 3).reshape(row_blocks * tile_edge, column_blocks * tile_edge)


def reduce_whole(partial_rows):
    return lax.psum_scatter(
        partial_rows.astype(jnp.bfloat16), "col", scatter_dimension=0, tiled=True
    ).astype(jnp.float32)


def shards(adjacency_tiles, tile_rows, tile_cols, tile_counts, features, weight):
    local_tiles = adjacency_tiles[0, 0]
    local_rows = tile_rows[0, 0]
    local_cols = tile_cols[0, 0]
    local_count = tile_counts[0, 0]
    tile_edge = local_tiles.shape[1]
    column_blocks = features.shape[0] // tile_edge
    row_blocks = column_blocks * lax.axis_size("col") // lax.axis_size("row")
    dense_block = densify(
        local_tiles, local_rows, local_cols, local_count, row_blocks, column_blocks
    )
    whole = lax.all_gather(features, "row", axis=1, tiled=True)
    partial_value = jnp.dot(dense_block, whole, preferred_element_type=jnp.float32)
    summed = reduce_whole(partial_value.astype(jnp.bfloat16).astype(jnp.float32))
    aggregated = summed.astype(jnp.bfloat16)
    full_weight = lax.all_gather(weight, "col", axis=0, tiled=True)
    hidden = jnp.dot(aggregated, full_weight, preferred_element_type=jnp.float32)
    return jnp.maximum(hidden, 0.0).astype(jnp.bfloat16)


def layer_kernel(
    inv, adj_hbm, feat_hbm, w_hbm, out_ref,
    adj, dense, feat, wfull, psend, own, yr, zr, acc, hidden,
    lsem, fsend, frecv, wsend, wrecv, vsend, vrecv, ysend, yrecv, zsend, zrecv,
):
    p, q = lax.axis_index("row"), lax.axis_index("col")
    y, z = q % 2, q // 2
    mate = p + 1 - 2 * (p % 2)
    across = (p + 2) % 4
    slots = adj_hbm.shape[0]
    tb = adj_hbm.shape[1]
    quarter = wfull.shape[2]

    cp_adj = pltpu.make_async_copy(adj_hbm, adj.at[pl.ds(0, slots)], lsem.at[0])
    cp_adj.start()
    cp_feat = pltpu.make_async_copy(feat_hbm, feat.at[0], lsem.at[1])
    cp_feat.start()
    w_mine = w_hbm.at[pl.ds(pl.multiple_of(p * quarter, quarter), quarter)]
    cp_w = pltpu.make_async_copy(w_mine, wfull.at[q, p], lsem.at[2])
    cp_w.start()

    barrier = pltpu.get_barrier_semaphore()
    for step in range(1, 8):
        pl.semaphore_signal(barrier, inc=1, device_id={"col": (q + step) % 8}, device_id_type=MESH)
    pl.semaphore_signal(barrier, inc=1, device_id={"row": mate}, device_id_type=MESH)
    pl.semaphore_signal(barrier, inc=1, device_id={"row": across}, device_id_type=MESH)
    pl.semaphore_wait(barrier, 9)

    def row_copy(src, dst, ssem, rsem, to):
        return pltpu.make_async_remote_copy(
            src_ref=src, dst_ref=dst, send_sem=ssem, recv_sem=rsem,
            device_id={"row": to}, device_id_type=MESH)

    def col_copy(src, dst, ssem, rsem, to):
        return pltpu.make_async_remote_copy(
            src_ref=src, dst_ref=dst, send_sem=ssem, recv_sem=rsem,
            device_id={"col": to}, device_id_type=MESH)

    f_mate = row_copy(feat_hbm, feat.at[1], fsend.at[0], frecv.at[0], mate)
    f_across = row_copy(feat_hbm, feat.at[2], fsend.at[1], frecv.at[1], across)
    f_fwd = row_copy(feat.at[2], feat.at[3], fsend.at[2], frecv.at[2], mate)
    f_mate.start()
    f_across.start()
    w_out = [
        col_copy(w_mine, wfull.at[q, p], wsend.at[step - 1], wrecv.at[step - 1], (q + step) % 8)
        for step in range(1, 8)
    ]
    for copy in w_out:
        copy.start()
    v_mate = row_copy(wfull.at[:, p], wfull.at[:, p], vsend.at[0], vrecv.at[0], mate)
    v_across = row_copy(wfull.at[:, p], wfull.at[:, p], vsend.at[1], vrecv.at[1], across)
    v_fwd = row_copy(wfull.at[:, across], wfull.at[:, across], vsend.at[2], vrecv.at[2], mate)

    adj[slots] = jnp.zeros((tb, tb), jnp.bfloat16)
    cp_adj.wait()

    @pl.loop(0, 8)
    def _(chunk):
        for half in range(2):
            for cb in range(8):
                dense[chunk % 2, chunk // 2, half * tb:(half + 1) * tb, cb * tb:(cb + 1) * tb] = adj[
                    inv[chunk * 16 + half * 8 + cb]]

    power = (1 + 3 * (z % 2)) * (1 + 15 * (z // 2))

    def dest(step):
        code = 15 * ((3 - step) // 3) + 90 * ((step % 3) % 2) + 177 * ((step % 3) // 2)
        code = code + 228 * (step // 3)
        return (code // power) % 4

    def y_copy(k, d):
        return col_copy(psend.at[k, d], yr.at[k, d], ysend.at[k, d], yrecv.at[k, d], 2 * z + 1 - y)

    def z_copy(k, d):
        side = (d - z + 4) // 4
        return col_copy(own.at[k, d], zr.at[side, k, d], zsend.at[k, d], zrecv.at[side, k, d],
                        q + 4 * side - 2)

    def product(k, side):
        rows = dense[side].reshape(4 * dense.shape[2], dense.shape[3])
        whole = jnp.dot(rows, feat[k], preferred_element_type=jnp.float32)
        return whole.astype(jnp.bfloat16).reshape(psend.shape[1:])

    def compute(k):
        psend[k] = product(k, 1 - y)

        @pl.loop(0, 4)
        def _(step):
            y_copy(k, dest(step)).start()

        own[k] = product(k, y)

    def reduce(k, step):
        d = dest(step)
        side = (d - z + 4) // 4
        up = z + 1 - 2 * side
        y_copy(k, d).wait_recv()
        has_up = (up + 1) % 5 > 0

        @pl.when(has_up)
        def _():
            z_copy(k, d).wait_recv()
            own[k, d] = (own[k, d].astype(jnp.float32) + yr[k, d].astype(jnp.float32)
                         + zr[side, k, d].astype(jnp.float32)).astype(jnp.bfloat16)

        @pl.when(jnp.logical_not(has_up))
        def _():
            own[k, d] = (own[k, d].astype(jnp.float32)
                         + yr[k, d].astype(jnp.float32)).astype(jnp.bfloat16)

        z_copy(k, d).start()

    def settle(k):
        y_copy(k, z).wait_recv()
        acc[...] = own[k, z].astype(jnp.float32) + yr[k, z].astype(jnp.float32)

        for side in (0, 1):
            @pl.when(z < 3 if side == 0 else z > 0)
            def _():
                col_copy(own.at[k, z], zr.at[side, k, z], zsend.at[k, z], zrecv.at[side, k, z],
                         2 * z + 1 - y).wait_recv()
                acc[...] += zr[side, k, z].astype(jnp.float32)

    panels = (p, mate, across, (mate + 2) % 4)

    def finish(k):
        rows = wfull[pl.ds(2 * panels[k], 2)].reshape(8 * quarter, wfull.shape[3])
        term = jnp.dot(acc[...].astype(jnp.bfloat16), rows, preferred_element_type=jnp.float32)
        if k == 0:
            hidden[...] = term
        elif k < 3:
            hidden[...] += term
        else:
            out_ref[...] = jnp.maximum(hidden[...] + term, 0.0).astype(jnp.bfloat16)

    cp_feat.wait()
    compute(0)
    f_mate.wait_recv()
    compute(1)
    cp_w.wait()
    for copy in w_out:
        copy.wait_recv()
    f_across.wait_recv()
    f_fwd.start()
    v_mate.start()
    v_across.start()
    for step in range(3):
        reduce(0, step)
    compute(2)
    v_across.wait_recv()
    v_fwd.start()
    reduce(1, 0)
    f_fwd.wait_recv()
    compute(3)
    reduce(1, 1)
    reduce(1, 2)
    v_mate.wait_recv()
    v_fwd.wait_recv()
    reduce(2, 0)
    settle(0)
    finish(0)
    reduce(2, 1)
    reduce(2, 2)
    reduce(3, 0)
    settle(1)
    finish(1)
    reduce(3, 1)
    reduce(3, 2)
    settle(2)
    finish(2)
    settle(3)
    finish(3)

    for copy in [f_mate, f_across, f_fwd, v_mate, v_across, v_fwd] + w_out:
        copy.wait_send()
    for k in range(4):
        @pl.loop(0, 4)
        def _(step):
            y_copy(k, dest(step)).wait_send()

        @pl.loop(0, 3)
        def _(step):
            z_copy(k, dest(step)).wait_send()


def fused_shards(adjacency_tiles, tile_rows, tile_cols, tile_counts, features, weight):
    tiles = adjacency_tiles[0, 0]
    slots, tb = tiles.shape[:2]
    live = jnp.arange(slots, dtype=jnp.int32)
    key = tile_rows[0, 0] * 8 + tile_cols[0, 0]
    place = jnp.arange(128, dtype=jnp.int32)
    hit = (place[:, None] == key[None, :]) & (live[None, :] < tile_counts[0, 0])
    inv = jnp.min(jnp.where(hit, live[None, :], slots), axis=1)
    width = features.shape[1]
    wide = weight.shape[1]
    bf = jnp.bfloat16
    dma = pltpu.SemaphoreType.DMA
    blocks = (4, 4, 256, width)
    return pl.pallas_call(
        layer_kernel,
        out_shape=jax.ShapeDtypeStruct((256, wide), bf),
        in_specs=[pl.BlockSpec(memory_space=pltpu.SMEM)]
        + [pl.BlockSpec(memory_space=pl.ANY)] * 3,
        out_specs=pl.BlockSpec(memory_space=pltpu.VMEM),
        scratch_shapes=[
            pltpu.VMEM((slots + 1, tb, tb), bf),
            pltpu.VMEM((2, 4, 256, 1024), bf),
            pltpu.VMEM((4, 1024, width), bf),
            pltpu.VMEM((8, 4, weight.shape[0] // 4, wide), bf),
            pltpu.VMEM(blocks, bf),
            pltpu.VMEM(blocks, bf),
            pltpu.VMEM(blocks, bf),
            pltpu.VMEM((2,) + blocks, bf),
            pltpu.VMEM((256, width), jnp.float32),
            pltpu.VMEM((256, wide), jnp.float32),
            dma((3,)),
            dma((3,)), dma((3,)),
            dma((7,)), dma((7,)),
            dma((3,)), dma((3,)),
            dma((4, 4)), dma((4, 4)),
            dma((4, 4)), dma((2, 4, 4)),
        ],
        compiler_params=pltpu.CompilerParams(
            collective_id=0, has_side_effects=True, vmem_limit_bytes=48 * 2**20),
    )(inv, tiles, features, weight)


def solution(mesh):
    fits = mesh.shape["row"] == 4 and mesh.shape["col"] == 8
    return jax.shard_map(
        fused_shards if fits else shards,
        mesh=mesh,
        in_specs=(
            P("row", "col", None, None, None),
            P("row", "col", None),
            P("row", "col", None),
            P("row", "col"),
            P("col", "row"),
            P("col", None),
        ),
        out_specs=P(("row", "col"), None),
        check_vma=False,
    )
```

```python
import functools

import jax
import jax.numpy as jnp
from jax import lax
from jax.experimental import pallas as pl
from jax.experimental.pallas import tpu as pltpu
from jax.sharding import PartitionSpec as P

MESH = pl.DeviceIdType.MESH


def densify(adjacency_tiles, tile_rows, tile_cols, tile_count, row_blocks, column_blocks):
    slots = adjacency_tiles.shape[0]
    tile_edge = adjacency_tiles.shape[1]
    live_mask = (jnp.arange(slots, dtype=jnp.int32) < tile_count).astype(jnp.bfloat16)
    masked = adjacency_tiles * live_mask[:, None, None]
    grid = jnp.zeros((row_blocks, column_blocks, tile_edge, tile_edge), jnp.bfloat16)
    grid = grid.at[tile_rows, tile_cols].add(masked)
    return grid.transpose(0, 2, 1, 3).reshape(row_blocks * tile_edge, column_blocks * tile_edge)


def reduce_whole(partial_rows):
    return lax.psum_scatter(
        partial_rows.astype(jnp.bfloat16), "col", scatter_dimension=0, tiled=True
    ).astype(jnp.float32)


def shards(adjacency_tiles, tile_rows, tile_cols, tile_counts, features, weight):
    local_tiles = adjacency_tiles[0, 0]
    local_rows = tile_rows[0, 0]
    local_cols = tile_cols[0, 0]
    local_count = tile_counts[0, 0]
    tile_edge = local_tiles.shape[1]
    column_blocks = features.shape[0] // tile_edge
    row_blocks = column_blocks * lax.axis_size("col") // lax.axis_size("row")
    dense_block = densify(
        local_tiles, local_rows, local_cols, local_count, row_blocks, column_blocks
    )
    whole = lax.all_gather(features, "row", axis=1, tiled=True)
    partial_value = jnp.dot(dense_block, whole, preferred_element_type=jnp.float32)
    summed = reduce_whole(partial_value.astype(jnp.bfloat16).astype(jnp.float32))
    aggregated = summed.astype(jnp.bfloat16)
    full_weight = lax.all_gather(weight, "col", axis=0, tiled=True)
    hidden = jnp.dot(aggregated, full_weight, preferred_element_type=jnp.float32)
    return jnp.maximum(hidden, 0.0).astype(jnp.bfloat16)


def layer_kernel(
    inv, adj_hbm, feat_hbm, w_hbm, out_ref,
    adj, dense, feat, wfull, psend, own, yr, zr, acc, hidden,
    lsem, fsend, frecv, wsend, wrecv, vsend, vrecv, ysend, yrecv, zsend, zrecv,
):
    p, q = lax.axis_index("row"), lax.axis_index("col")
    y, z = q % 2, q // 2
    mate = p + 1 - 2 * (p % 2)
    across = (p + 2) % 4
    slots = adj_hbm.shape[0]
    tb = adj_hbm.shape[1]
    quarter = wfull.shape[2]

    cp_adj = pltpu.make_async_copy(adj_hbm, adj.at[pl.ds(0, slots)], lsem.at[0])
    cp_adj.start()
    cp_feat = pltpu.make_async_copy(feat_hbm, feat.at[0], lsem.at[1])
    cp_feat.start()
    w_mine = w_hbm.at[pl.ds(pl.multiple_of(p * quarter, quarter), quarter)]
    cp_w = pltpu.make_async_copy(w_mine, wfull.at[q, p], lsem.at[2])
    cp_w.start()

    barrier = pltpu.get_barrier_semaphore()
    for step in range(1, 8):
        pl.semaphore_signal(barrier, inc=1, device_id={"col": (q + step) % 8}, device_id_type=MESH)
    pl.semaphore_signal(barrier, inc=1, device_id={"row": mate}, device_id_type=MESH)
    pl.semaphore_signal(barrier, inc=1, device_id={"row": across}, device_id_type=MESH)
    pl.semaphore_wait(barrier, 9)

    def row_copy(src, dst, ssem, rsem, to):
        return pltpu.make_async_remote_copy(
            src_ref=src, dst_ref=dst, send_sem=ssem, recv_sem=rsem,
            device_id={"row": to}, device_id_type=MESH)

    def col_copy(src, dst, ssem, rsem, to):
        return pltpu.make_async_remote_copy(
            src_ref=src, dst_ref=dst, send_sem=ssem, recv_sem=rsem,
            device_id={"col": to}, device_id_type=MESH)

    f_mate = row_copy(feat_hbm, feat.at[1], fsend.at[0], frecv.at[0], mate)
    f_across = row_copy(feat_hbm, feat.at[2], fsend.at[1], frecv.at[1], across)
    f_fwd = row_copy(feat.at[2], feat.at[3], fsend.at[2], frecv.at[2], mate)
    f_mate.start()
    f_across.start()
    w_out = [
        col_copy(w_mine, wfull.at[q, p], wsend.at[step - 1], wrecv.at[step - 1], (q + step) % 8)
        for step in range(1, 8)
    ]
    for copy in w_out:
        copy.start()
    v_mate = row_copy(wfull.at[:, p], wfull.at[:, p], vsend.at[0], vrecv.at[0], mate)
    v_across = row_copy(wfull.at[:, p], wfull.at[:, p], vsend.at[1], vrecv.at[1], across)
    v_fwd = row_copy(wfull.at[:, across], wfull.at[:, across], vsend.at[2], vrecv.at[2], mate)

    adj[slots] = jnp.zeros((tb, tb), jnp.bfloat16)
    cp_adj.wait()

    def place(side):
        @pl.loop(0, 4)
        def _(d):
            for half in range(2):
                for cb in range(8):
                    dense[side, d, half * tb:(half + 1) * tb, cb * tb:(cb + 1) * tb] = adj[
                        inv[(2 * d + side) * 16 + half * 8 + cb]]

    power = (1 + 3 * (z % 2)) * (1 + 15 * (z // 2))

    def dest(step):
        code = 15 * ((3 - step) // 3) + 90 * ((step % 3) % 2) + 177 * ((step % 3) // 2)
        code = code + 228 * (step // 3)
        return (code // power) % 4

    def y_copy(k, d):
        return col_copy(psend.at[k, d], yr.at[k, d], ysend.at[k, d], yrecv.at[k, d], 2 * z + 1 - y)

    def z_copy(k, d):
        side = (d - z + 4) // 4
        return col_copy(own.at[k, d], zr.at[side, k, d], zsend.at[k, d], zrecv.at[side, k, d],
                        q + 4 * side - 2)

    def product(k, side):
        rows = dense[side].reshape(4 * dense.shape[2], dense.shape[3])
        whole = jnp.dot(rows, feat[k], preferred_element_type=jnp.float32)
        return whole.astype(jnp.bfloat16).reshape(psend.shape[1:])

    def compute(k):
        if k == 0:
            @pl.loop(0, 4)
            def _(step):
                d = dest(step)
                psend[k, d] = jnp.dot(dense[1 - y, d], feat[k],
                                      preferred_element_type=jnp.float32).astype(jnp.bfloat16)
                y_copy(k, d).start()

            place(y)
        else:
            psend[k] = product(k, 1 - y)

            @pl.loop(0, 4)
            def _(step):
                y_copy(k, dest(step)).start()

        own[k] = product(k, y)

    def reduce(k, step):
        d = dest(step)
        side = (d - z + 4) // 4
        up = z + 1 - 2 * side
        y_copy(k, d).wait_recv()
        has_up = (up + 1) % 5 > 0

        @pl.when(has_up)
        def _():
            z_copy(k, d).wait_recv()
            own[k, d] = (own[k, d].astype(jnp.float32) + yr[k, d].astype(jnp.float32)
                         + zr[side, k, d].astype(jnp.float32)).astype(jnp.bfloat16)

        @pl.when(jnp.logical_not(has_up))
        def _():
            own[k, d] = (own[k, d].astype(jnp.float32)
                         + yr[k, d].astype(jnp.float32)).astype(jnp.bfloat16)

        z_copy(k, d).start()

    def settle(k):
        y_copy(k, z).wait_recv()
        acc[...] = own[k, z].astype(jnp.float32) + yr[k, z].astype(jnp.float32)

        for side in (0, 1):
            @pl.when(z < 3 if side == 0 else z > 0)
            def _():
                col_copy(own.at[k, z], zr.at[side, k, z], zsend.at[k, z], zrecv.at[side, k, z],
                         2 * z + 1 - y).wait_recv()
                acc[...] += zr[side, k, z].astype(jnp.float32)

    panels = (p, mate, across, (mate + 2) % 4)

    def finish(k):
        rows = wfull[pl.ds(2 * panels[k], 2)].reshape(8 * quarter, wfull.shape[3])
        term = jnp.dot(acc[...].astype(jnp.bfloat16), rows, preferred_element_type=jnp.float32)
        if k == 0:
            hidden[...] = term
        elif k < 3:
            hidden[...] += term
        else:
            out_ref[...] = jnp.maximum(hidden[...] + term, 0.0).astype(jnp.bfloat16)

    place(1 - y)
    cp_feat.wait()
    compute(0)
    f_mate.wait_recv()
    compute(1)
    cp_w.wait()
    for copy in w_out:
        copy.wait_recv()
    f_across.wait_recv()
    f_fwd.start()
    v_mate.start()
    v_across.start()
    for step in range(3):
        reduce(0, step)
    compute(2)
    v_across.wait_recv()
    v_fwd.start()
    reduce(1, 0)
    f_fwd.wait_recv()
    compute(3)
    reduce(1, 1)
    reduce(1, 2)
    v_mate.wait_recv()
    v_fwd.wait_recv()
    reduce(2, 0)
    settle(0)
    finish(0)
    reduce(2, 1)
    reduce(2, 2)
    reduce(3, 0)
    settle(1)
    finish(1)
    reduce(3, 1)
    reduce(3, 2)
    settle(2)
    finish(2)
    settle(3)
    finish(3)

    for copy in [f_mate, f_across, f_fwd, v_mate, v_across, v_fwd] + w_out:
        copy.wait_send()
    for k in range(4):
        @pl.loop(0, 4)
        def _(step):
            y_copy(k, dest(step)).wait_send()

        @pl.loop(0, 3)
        def _(step):
            z_copy(k, dest(step)).wait_send()


def fused_shards(adjacency_tiles, tile_rows, tile_cols, tile_counts, features, weight):
    tiles = adjacency_tiles[0, 0]
    slots, tb = tiles.shape[:2]
    live = jnp.arange(slots, dtype=jnp.int32)
    key = tile_rows[0, 0] * 8 + tile_cols[0, 0]
    place = jnp.arange(128, dtype=jnp.int32)
    hit = (place[:, None] == key[None, :]) & (live[None, :] < tile_counts[0, 0])
    inv = jnp.min(jnp.where(hit, live[None, :], slots), axis=1)
    width = features.shape[1]
    wide = weight.shape[1]
    bf = jnp.bfloat16
    dma = pltpu.SemaphoreType.DMA
    blocks = (4, 4, 256, width)
    return pl.pallas_call(
        layer_kernel,
        out_shape=jax.ShapeDtypeStruct((256, wide), bf),
        in_specs=[pl.BlockSpec(memory_space=pltpu.SMEM)]
        + [pl.BlockSpec(memory_space=pl.ANY)] * 3,
        out_specs=pl.BlockSpec(memory_space=pltpu.VMEM),
        scratch_shapes=[
            pltpu.VMEM((slots + 1, tb, tb), bf),
            pltpu.VMEM((2, 4, 256, 1024), bf),
            pltpu.VMEM((4, 1024, width), bf),
            pltpu.VMEM((8, 4, weight.shape[0] // 4, wide), bf),
            pltpu.VMEM(blocks, bf),
            pltpu.VMEM(blocks, bf),
            pltpu.VMEM(blocks, bf),
            pltpu.VMEM((2,) + blocks, bf),
            pltpu.VMEM((256, width), jnp.float32),
            pltpu.VMEM((256, wide), jnp.float32),
            dma((3,)),
            dma((3,)), dma((3,)),
            dma((7,)), dma((7,)),
            dma((3,)), dma((3,)),
            dma((4, 4)), dma((4, 4)),
            dma((4, 4)), dma((2, 4, 4)),
        ],
        compiler_params=pltpu.CompilerParams(
            collective_id=0, has_side_effects=True, vmem_limit_bytes=48 * 2**20),
    )(inv, tiles, features, weight)


def solution(mesh):
    fits = mesh.shape["row"] == 4 and mesh.shape["col"] == 8
    return jax.shard_map(
        fused_shards if fits else shards,
        mesh=mesh,
        in_specs=(
            P("row", "col", None, None, None),
            P("row", "col", None),
            P("row", "col", None),
            P("row", "col"),
            P("col", "row"),
            P("col", None),
        ),
        out_specs=P(("row", "col"), None),
        check_vma=False,
    )
```
